128 devices in a mesh: groups: 4 (over y), shards: 8 (over z, x_lo), tensor: 4 (over x_hi, core).
Axes of the slice: x: 4 (x_hi: 2, x_lo: 2; x = x_hi * 2 + x_lo), y: 4, z: 4, core: 2. Of those that a mesh axis runs over, the one named last changes fastest.
Arguments:
- global_layer: float32 [3, 2816, 1024], P(None, 'tensor', 'shards'), may hold values from -6 to 6
- local_layer: bfloat16 [4, 3, 2816, 1024], P('groups', None, 'tensor', 'shards'), may hold values from -6 to 6
- layer_momentum: float32 [3, 2816, 1024], P(None, 'tensor', 'shards'), may hold values from -6 to 6
- global_embed: float32 [32000, 1024], P('shards', 'tensor'), may hold values from -6 to 6
- local_embed: bfloat16 [4, 32000, 1024], P('groups', 'shards', 'tensor'), may hold values from -6 to 6
- embed_momentum: float32 [32000, 1024], P('shards', 'tensor'), may hold values from -6 to 6
- projection: float32 [1024, 64], P('tensor'), may hold values from -0.1875 to 0.1875
Outputs:
- new_layer: float32 [3, 2816, 1024], P(None, 'tensor', 'shards')
- new_layer_momentum: float32 [3, 2816, 1024], P(None, 'tensor', 'shards')
- new_embed: float32 [32000, 1024], P('shards', 'tensor')
- new_embed_momentum: float32 [32000, 1024], P('shards', 'tensor')
The draws below stay inside these ranges and needn't reach their ends.
All inputs are finite; a program needn't handle non-finite values.
Results may differ from the reference program's by a relative error of at most 0.0003.
Values sent between devices are 32-bit elements; how exact they have to be, the bound alone decides.
A program may use at most 128 MiB of HBM per device.

```python
import jax
import jax.numpy as jnp
from jax import lax

D = 1024
FF = 2816
VOCAB = 32000
RANK = 64
LAYERS = 1
GROUPS = 4
N_GROUPS = 4


def shard_levels(key, shape, cuts, smallest, high):
    gain = 1.0
    for axis_at, parts in cuts:
        steps = jax.random.uniform(jax.random.fold_in(jax.random.fold_in(key, 6), axis_at), (parts,), jnp.float32, smallest / len(cuts), high / len(cuts))
        gain = gain * jnp.repeat(jnp.exp(steps), shape[axis_at] // parts).reshape((-1,) + (1,) * (len(shape) - 1 - axis_at))
    return gain


def noise(rng, shape, spread, bound, cuts=(), dtype=jnp.bfloat16):
    entries = spread * jax.random.normal(rng, shape, jnp.float32)
    if cuts:
        entries = entries * shard_levels(rng, shape, cuts, -0.22, 0.18)
    return jnp.clip(entries, -bound, bound).astype(dtype)


def setup_inputs(seed: int = 0) -> dict:
    key_list = jax.random.split(jax.random.key(seed), 8)
    global_layer = noise(key_list[0], (3 * LAYERS, FF, D), 1.0, 6.0, ((1, 4), (2, 8)), jnp.float32)
    local_layer = noise(key_list[1], (GROUPS, 3 * LAYERS, FF, D), 1.0, 6.0, ((0, 4), (2, 4), (3, 8)))
    layer_momentum = noise(key_list[2], (3 * LAYERS, FF, D), 0.5, 6.0, ((1, 4), (2, 8)), jnp.float32)
    global_embed = noise(key_list[3], (VOCAB, D), 1.0, 6.0, ((0, 8), (1, 4)), jnp.float32)
    local_embed = noise(key_list[4], (GROUPS, VOCAB, D), 1.0, 6.0, ((0, 4), (1, 8), (2, 4)))
    embed_momentum = noise(key_list[5], (VOCAB, D), 0.5, 6.0, ((0, 8), (1, 4)), jnp.float32)
    projection = noise(key_list[6], (D, RANK), D ** -0.5, 0.1875, ((0, 4),), jnp.float32)
    return {"global_layer": global_layer, "local_layer": local_layer, "layer_momentum": layer_momentum, "global_embed": global_embed, "local_embed": local_embed, "embed_momentum": embed_momentum, "projection": projection}


momentum_rate = 0.9
outer_rate = 0.7


def reference(global_layer, local_layer, layer_momentum, global_embed, local_embed, embed_momentum, projection):
    layer_total = jnp.zeros(global_layer.shape, jnp.float32)
    for group in range(N_GROUPS):
        layer_total = layer_total + (global_layer - local_layer[group].astype(jnp.float32))
    layer_delta = layer_total / N_GROUPS
    new_layer_momentum = momentum_rate * layer_momentum + layer_delta
    new_layer = global_layer - outer_rate * (layer_delta + momentum_rate * new_layer_momentum)
    projected = jnp.zeros((global_embed.shape[0], projection.shape[1]), jnp.float32)
    for group in range(N_GROUPS):
        difference = global_embed - local_embed[group].astype(jnp.float32)
        projected = projected + jnp.dot(difference, projection, precision=lax.Precision.HIGHEST, preferred_element_type=jnp.float32)
    projected = projected / N_GROUPS
    embed_delta = jnp.dot(projected, projection.T, precision=lax.Precision.HIGHEST, preferred_element_type=jnp.float32)
    new_embed_momentum = momentum_rate * embed_momentum + embed_delta
    new_embed = global_embed - outer_rate * (embed_delta + momentum_rate * new_embed_momentum)
    return new_layer, new_layer_momentum, new_embed, new_embed_momentum
```

```python
import functools

import jax
import jax.numpy as jnp
from jax import lax
from jax.experimental import pallas as pl
from jax.experimental.pallas import tpu as pltpu
from jax.sharding import PartitionSpec as P

MESH = pl.DeviceIdType.MESH
F32 = jnp.float32
BF16 = jnp.bfloat16

momentum_rate = 0.9
outer_rate = 0.7

LROWS = 2112
LC = 3
LU = 88
EC = 2
EU = 64
CORE_ROWS = EC * 2 * 4 * EU
VALID = 1000


def nesterov(weights, momentum, delta):
    moved = momentum_rate * momentum + delta
    return weights - outer_rate * (delta + momentum_rate * moved), moved


def split(value):
    high = value.astype(BF16)
    return high, (value - high.astype(F32)).astype(BF16)


def dot_t(a, b):
    return lax.dot_general(a, b, (((1,), (1,)), ((), ())), preferred_element_type=F32)


def dot(a, b):
    return jnp.dot(a, b, preferred_element_type=F32)


def kernel(
    ll, gl, lm, le, ge, em, pt,
    nl, nlm, ne, nem,
    vll, vgl, vlm, vle, vge, vem, vpt, w,
    lacc, lr1, lr2, lsum,
    pk, er0, er1, er2, erx, esum,
    load_sem, le_sem, ge_sem, lsend, lrecv, esend, erecv, xsend, xrecv, csend, crecv,
):
    y = lax.axis_index("groups")
    t = lax.axis_index("tensor")
    core = lax.rem(t, 2)
    x_hi = lax.div(t, 2)
    flip = y + 1 - 2 * lax.rem(y, 2)
    mirror = 3 - y
    bit_b = lax.div(y, 2)
    bit_a = lax.rem(bit_b + y, 2)
    plan = (((flip, bit_a), (mirror, bit_b)), ((mirror, bit_b), (flip, bit_a)))
    other_core = {"tensor": x_hi * 2 + 1 - core}
    other_x = {"tensor": (1 - x_hi) * 2 + core}

    def rows(ref, start, size):
        return ref.at[pl.ds(pl.multiple_of(start, 8), size)]

    loads = [
        pltpu.make_async_copy(src, dst, load_sem.at[i])
        for i, (src, dst) in enumerate(((ll, vll), (pt, vpt), (gl, vgl), (lm, vlm), (em, vem)))
    ]
    piece = ((0, 512), (512, VALID - 512))
    eloads = {}
    for turn in range(2):
        k = (1 - core) if turn == 0 else core
        for c in range(EC):
            start, size = piece[c]
            for side in range(2):
                src = pl.ds(pl.multiple_of(side * 2000 + k * VALID + start, 8), size)
                dst = (side * 2 + k, pl.ds(start, size))
                i = (turn * EC + c) * 2 + side
                eloads[turn, c, side] = (
                    pltpu.make_async_copy(le.at[src], vle.at[dst], le_sem.at[i]),
                    pltpu.make_async_copy(ge.at[src], vge.at[dst], ge_sem.at[i]),
                )
    loads[0].start()
    loads[1].start()
    for c in range(EC):
        for turn in range(2):
            for side in range(2):
                for copy in eloads[turn, c, side]:
                    copy.start()
    for copy in loads[2:]:
        copy.start()

    barrier = pltpu.get_barrier_semaphore()
    for where in ({"groups": flip}, {"groups": mirror}, other_core, other_x):
        pl.semaphore_signal(barrier, inc=1, device_id=where, device_id_type=MESH)

    for q in range(4):
        vge[q, VALID:, :] = jnp.zeros((CORE_ROWS - VALID, 256), F32)
        vle[q, VALID:, :] = jnp.zeros((CORE_ROWS - VALID, 256), BF16)

    loads[0].wait()
    lacc[...] = vll[...].astype(F32)
    loads[1].wait()
    high, low = split(vpt[...])
    none = jnp.zeros((64, 256), BF16)
    w[0] = jnp.concatenate([high, none], axis=0)
    w[1] = jnp.concatenate([low, none], axis=0)
    w[2] = jnp.concatenate([none, high], axis=0)
    w[3] = jnp.concatenate([none, low], axis=0)
    pl.semaphore_wait(barrier, 4)

    started = []

    def send(src, dst, send_sem, recv_sem, where):
        copy = pltpu.make_async_remote_copy(
            src_ref=src, dst_ref=dst, send_sem=send_sem, recv_sem=recv_sem,
            device_id=where, device_id_type=MESH,
        )
        copy.start()
        started.append(copy)
        return copy

    lcopies = {}

    def lunit(h, c, f1, f2):
        return ((h * LC + c) * 4 + f1 * 2 + f2) * LU

    def lstage(stage, h, c):
        (p1, f1), (p2, f2) = plan[h]
        n = h * LC + c
        i = n * 4 + stage
        if stage == 0:
            src, dst, p = rows(lacc, lunit(h, c, 1 - f1, 0), 2 * LU), lr1.at[pl.ds(n * 2 * LU, 2 * LU)], p1
        elif stage == 1:
            src, dst, p = rows(lacc, lunit(h, c, f1, 1 - f2), LU), lr2.at[pl.ds(n * LU, LU)], p2
        elif stage == 2:
            src = dst = rows(lsum, lunit(h, c, f1, f2), LU)
            p = p2
        else:
            src = dst = rows(lsum, lunit(h, c, f1, 0), 2 * LU)
            p = p1
        lcopies[stage, h, c] = send(src, dst, lsend.at[i], lrecv.at[i], {"groups": p})

    ecopies = {}

    def eunit(k, c, h, f1, f2):
        return (((k * EC + c) * 2 + h) * 4 + f1 * 2 + f2) * EU

    def estage(stage, c, h):
        (p1, f1), (p2, f2) = plan[h]
        n = c * 2 + h
        i = n * 4 + stage
        if stage == 0:
            src, dst, p = rows(pk, eunit(core, c, h, 1 - f1, 0), 2 * EU), er1.at[pl.ds(n * 2 * EU, 2 * EU)], p1
        elif stage == 1:
            src, dst, p = rows(pk, eunit(core, c, h, f1, 1 - f2), EU), er2.at[pl.ds(n * EU, EU)], p2
        elif stage == 2:
            src = dst = rows(esum, eunit(core, c, h, f1, f2), EU)
            p = p2
        else:
            src = dst = rows(esum, eunit(core, c, h, f1, 0), 2 * EU)
            p = p1
        ecopies[stage, c, h] = send(src, dst, esend.at[i], erecv.at[i], {"groups": p})

    def project(k, c):
        @pl.loop(0, 4)
        def _(step):
            start = pl.multiple_of(c * 512 + step * 128, 128)
            total = None
            for side in range(2):
                q = side * 2 + k
                d = vge[q, pl.ds(start, 128), :] - vle[q, pl.ds(start, 128), :].astype(F32)
                dh, dl = split(d)
                part = dot_t(dh, w[side * 2]) + dot_t(dl, w[side * 2]) + dot_t(dh, w[side * 2 + 1])
                total = part if total is None else total + part
            pk[pl.ds(pl.multiple_of(k * CORE_ROWS + start, 128), 128), :] = total

    def finish(k, c, h):
        size = min(256, VALID - (c * 2 + h) * 256)
        start = (c * 2 + h) * 256
        value = esum[pl.ds(pl.multiple_of(k * CORE_ROWS + start, 8), size), :] * 0.25
        vh, vl = split(value)
        for side in range(2):
            delta = dot(vh, w[side * 2]) + dot(vl, w[side * 2]) + dot(vh, w[side * 2 + 1])
            out = pl.ds(pl.multiple_of(side * 2000 + k * VALID + start, 8), size)
            ne[out, :], nem[out, :] = nesterov(vge[side * 2 + k, pl.ds(start, size), :], vem[out, :], delta)

    for c in range(LC):
        for h in range(2):
            lstage(0, h, c)

    ccopies = {}
    for c in range(EC):
        for turn in range(2):
            k = (1 - core) if turn == 0 else core
            for side in range(2):
                for copy in eloads[turn, c, side]:
                    copy.wait()
            project(k, c)
            if turn == 0:
                ccopies[0, c] = send(
                    rows(pk, eunit(k, c, 0, 0, 0), 512), er0.at[pl.ds(c * 512, 512)],
                    csend.at[c], crecv.at[c], other_core,
                )
    for c in range(EC):
        ccopies[0, c].wait_recv()
        mine = pl.ds(pl.multiple_of(eunit(core, c, 0, 0, 0), 8), 512)
        pk[mine, :] += er0[pl.ds(c * 512, 512), :]
        for h in range(2):
            estage(0, c, h)

    for c in range(LC):
        for h in range(2):
            lcopies[0, h, c].wait_recv()
            f1 = plan[h][0][1]
            mine = pl.ds(pl.multiple_of(lunit(h, c, f1, 0), 8), 2 * LU)
            lacc[mine, :] += lr1[pl.ds((h * LC + c) * 2 * LU, 2 * LU), :]
            lstage(1, h, c)

    for c in range(EC):
        for h in range(2):
            ecopies[0, c, h].wait_recv()
            f1 = plan[h][0][1]
            mine = pl.ds(pl.multiple_of(eunit(core, c, h, f1, 0), 8), 2 * EU)
            pk[mine, :] += er1[pl.ds((c * 2 + h) * 2 * EU, 2 * EU), :]
            estage(1, c, h)

    xcopies = {}
    for c in range(EC):
        for h in range(2):
            ecopies[1, c, h].wait_recv()
            (_, f1), (_, f2) = plan[h]
            n = c * 2 + h
            start = eunit(core, c, h, f1, f2)
            mine = pl.ds(pl.multiple_of(start, 8), EU)
            pk[mine, :] += er2[pl.ds(n * EU, EU), :]
            xcopies[c, h] = send(
                rows(pk, start, EU), erx.at[pl.ds(n * EU, EU)], xsend.at[n], xrecv.at[n], other_x
            )

    for c in range(LC):
        for h in range(2):
            lcopies[1, h, c].wait_recv()
            (_, f1), (_, f2) = plan[h]
            mine = pl.ds(pl.multiple_of(lunit(h, c, f1, f2), 8), LU)
            lsum[mine, :] = lacc[mine, :] + lr2[pl.ds((h * LC + c) * LU, LU), :]
            lstage(2, h, c)

    for c in range(EC):
        for h in range(2):
            xcopies[c, h].wait_recv()
            (_, f1), (_, f2) = plan[h]
            n = c * 2 + h
            mine = pl.ds(pl.multiple_of(eunit(core, c, h, f1, f2), 8), EU)
            esum[mine, :] = pk[mine, :] + erx[pl.ds(n * EU, EU), :]
            estage(2, c, h)

    for c in range(EC):
        for h in range(2):
            ecopies[2, c, h].wait_recv()
            estage(3, c, h)

    for c in range(LC):
        for h in range(2):
            lcopies[2, h, c].wait_recv()
            lstage(3, h, c)

    for copy in loads[2:]:
        copy.wait()
    for c in range(EC):
        for h in range(2):
            ecopies[3, c, h].wait_recv()
            n = c * 2 + h
            whole = rows(esum, eunit(core, c, h, 0, 0), 4 * EU)
            ccopies[1, c, h] = send(whole, whole, csend.at[EC + n], crecv.at[EC + n], other_core)
            finish(core, c, h)
    for c in range(EC):
        for h in range(2):
            ccopies[1, c, h].wait_recv()
            finish(1 - core, c, h)

    for c in range(LC):
        for h in range(2):
            lcopies[3, h, c].wait_recv()
            block = pl.ds((h * LC + c) * 4 * LU, 4 * LU)
            weights = vgl[block, :]
            delta = weights - lsum[block, :] * 0.25
            nl[block, :], nlm[block, :] = nesterov(weights, vlm[block, :], delta)

    for copy in started:
        copy.wait_send()


def body(
    global_layer, local_layer, layer_momentum, global_embed, local_embed, embed_momentum, projection
):
    hbm = pl.BlockSpec(memory_space=pltpu.HBM)
    vmem = pl.BlockSpec(memory_space=pltpu.VMEM)
    dma = pltpu.SemaphoreType.DMA
    layer_shape = global_layer.shape
    nl, nlm, ne, nem = pl.pallas_call(
        kernel,
        out_shape=(
            pltpu.VMEM((LROWS, 128), F32),
            pltpu.VMEM((LROWS, 128), F32),
            pltpu.VMEM((4000, 256), F32),
            pltpu.VMEM((4000, 256), F32),
        ),
        in_specs=[hbm] * 7,
        out_specs=(vmem,) * 4,
        scratch_shapes=[
            pltpu.VMEM((LROWS, 128), BF16),
            pltpu.VMEM((LROWS, 128), F32),
            pltpu.VMEM((LROWS, 128), F32),
            pltpu.VMEM((4, CORE_ROWS, 256), BF16),
            pltpu.VMEM((4, CORE_ROWS, 256), F32),
            pltpu.VMEM((4000, 256), F32),
            pltpu.VMEM((64, 256), F32),
            pltpu.VMEM((4, 128, 256), BF16),
            pltpu.VMEM((LROWS, 128), F32),
            pltpu.VMEM((2 * LC * 2 * LU, 128), F32),
            pltpu.VMEM((2 * LC * LU, 128), F32),
            pltpu.VMEM((LROWS, 128), F32),
            pltpu.VMEM((2 * CORE_ROWS, 128), F32),
            pltpu.VMEM((CORE_ROWS, 128), F32),
            pltpu.VMEM((2 * EC * 2 * EU, 128), F32),
            pltpu.VMEM((2 * EC * EU, 128), F32),
            pltpu.VMEM((2 * EC * EU, 128), F32),
            pltpu.VMEM((2 * CORE_ROWS, 128), F32),
            dma((5,)),
            dma((4 * EC,)),
            dma((4 * EC,)),
            dma((2 * LC * 4,)),
            dma((2 * LC * 4,)),
            dma((2 * EC * 4,)),
            dma((2 * EC * 4,)),
            dma((2 * EC,)),
            dma((2 * EC,)),
            dma((3 * EC,)),
            dma((3 * EC,)),
        ],
        compiler_params=pltpu.CompilerParams(
            collective_id=0, has_side_effects=True, vmem_limit_bytes=40 * 1024 * 1024
        ),
    )(
        *(
            pltpu.with_memory_space_constraint(array, pltpu.HBM)
            for array in (
                local_layer.reshape(LROWS, 128),
                global_layer.reshape(LROWS, 128),
                layer_momentum.reshape(LROWS, 128),
                local_embed.reshape(4000, 256),
                global_embed,
                embed_momentum,
                projection.T,
            )
        )
    )
    return nl.reshape(layer_shape), nlm.reshape(layer_shape), ne, nem


def solution(mesh):
    in_specs = (
        P(None, "tensor", "shards"),
        P("groups", None, "tensor", "shards"),
        P(None, "tensor", "shards"),
        P("shards", "tensor"),
        P("groups", "shards", "tensor"),
        P("shards", "tensor"),
        P("tensor", None),
    )
    out_specs = (
        P(None, "tensor", "shards"),
        P(None, "tensor", "shards"),
        P("shards", "tensor"),
        P("shards", "tensor"),
    )
    return jax.shard_map(body, mesh=mesh, in_specs=in_specs, out_specs=out_specs, check_vma=False)
```

```python
import jax
import jax.numpy as jnp
from jax import lax
from jax.experimental import pallas as pl
from jax.experimental.pallas import tpu as pltpu
from jax.sharding import PartitionSpec as P

MESH = pl.DeviceIdType.MESH
F32 = jnp.float32
BF16 = jnp.bfloat16

momentum_rate = 0.9
outer_rate = 0.7

LROWS = 2112
LC = 3
LU = 88
EC = 2
EU = 64
CORE_ROWS = EC * 2 * 4 * EU
VALID = 1000


def nesterov(weights, momentum, delta):
    moved = momentum_rate * momentum + delta
    return weights - outer_rate * (delta + momentum_rate * moved), moved


def split(value):
    high = value.astype(BF16)
    return high, (value - high.astype(F32)).astype(BF16)


def dot_t(a, b):
    return lax.dot_general(a, b, (((1,), (1,)), ((), ())), preferred_element_type=F32)


def dot(a, b):
    return jnp.dot(a, b, preferred_element_type=F32)


def part(n):
    return n * 256, min(256, VALID - n * 256)


def piece_step(esum, w, vge, vem, k, side, start, size):
    value = esum[pl.ds(pl.multiple_of(k * CORE_ROWS + start, 8), size), :] * 0.25
    vh, vl = split(value)
    delta = dot(vh, w[side * 2]) + dot(vl, w[side * 2]) + dot(vh, w[side * 2 + 1])
    moment = vem[pl.ds(pl.multiple_of(side * 2000 + k * VALID + start, 8), size), :]
    return nesterov(vge[side * 2 + k, pl.ds(start, size), :], moment, delta)


def write_kernel(
    vgl, vlm, vge, vem, w, lsum, esum, one, onem,
    nl, nlm, ne, nem,
    snl, snlm, sne, snem, sem,
):
    core = lax.rem(lax.axis_index("tensor"), 2)
    started = []

    def put(src, dst):
        copy = pltpu.make_async_copy(src, dst, sem.at[len(started)])
        copy.start()
        started.append(copy)

    def place(k, side, start, size):
        return pl.ds(pl.multiple_of(side * 2000 + k * VALID + start, 8), size)

    for side in range(2):
        put(one.at[side], ne.at[place(core, side, 0, VALID)])
        put(onem.at[side], nem.at[place(core, side, 0, VALID)])
    for n in range(4):
        start, size = part(n)
        for side in range(2):
            rows = pl.ds(start, size)
            sne[side, rows, :], snem[side, rows, :] = piece_step(
                esum, w, vge, vem, 1 - core, side, start, size
            )
            put(sne.at[side, rows], ne.at[place(1 - core, side, start, size)])
            put(snem.at[side, rows], nem.at[place(1 - core, side, start, size)])
    for n in range(3):
        block = pl.ds(n * 704, 704)
        weights = vgl[block, :]
        delta = weights - lsum[block, :] * 0.25
        snl[block, :], snlm[block, :] = nesterov(weights, vlm[block, :], delta)
        put(snl.at[block], nl.at[block])
        put(snlm.at[block], nlm.at[block])
    for copy in started:
        copy.wait()


def kernel(
    ll, gl, lm, le, ge, em, pt,
    vgl, vlm, vge, vem, w, lsum, esum, one, onem,
    vll, vle, vpt,
    lacc, lr1, lr2,
    pk, er0, er1, er2, erx,
    load_sem, le_sem, ge_sem, lsend, lrecv, esend, erecv, xsend, xrecv, csend, crecv,
):
    y = lax.axis_index("groups")
    t = lax.axis_index("tensor")
    core = lax.rem(t, 2)
    x_hi = lax.div(t, 2)
    flip = y + 1 - 2 * lax.rem(y, 2)
    mirror = 3 - y
    bit_b = lax.div(y, 2)
    bit_a = lax.rem(bit_b + y, 2)
    plan = (((flip, bit_a), (mirror, bit_b)), ((mirror, bit_b), (flip, bit_a)))
    other_core = {"tensor": x_hi * 2 + 1 - core}
    other_x = {"tensor": (1 - x_hi) * 2 + core}

    def rows(ref, start, size):
        return ref.at[pl.ds(pl.multiple_of(start, 8), size)]

    loads = [
        pltpu.make_async_copy(src, dst, load_sem.at[i])
        for i, (src, dst) in enumerate(((ll, vll), (pt, vpt), (gl, vgl), (lm, vlm), (em, vem)))
    ]
    piece = ((0, 512), (512, VALID - 512))
    eloads = {}
    for turn in range(2):
        k = (1 - core) if turn == 0 else core
        for c in range(EC):
            start, size = piece[c]
            for side in range(2):
                src = pl.ds(pl.multiple_of(side * 2000 + k * VALID + start, 8), size)
                dst = (side * 2 + k, pl.ds(start, size))
                i = (turn * EC + c) * 2 + side
                eloads[turn, c, side] = (
                    pltpu.make_async_copy(le.at[src], vle.at[dst], le_sem.at[i]),
                    pltpu.make_async_copy(ge.at[src], vge.at[dst], ge_sem.at[i]),
                )
    loads[0].start()
    loads[1].start()
    for c in range(EC):
        for turn in range(2):
            for side in range(2):
                for copy in eloads[turn, c, side]:
                    copy.start()
    for copy in loads[2:]:
        copy.start()

    barrier = pltpu.get_barrier_semaphore()
    for where in ({"groups": flip}, {"groups": mirror}, other_core, other_x):
        pl.semaphore_signal(barrier, inc=1, device_id=where, device_id_type=MESH)

    for q in range(4):
        vge[q, VALID:, :] = jnp.zeros((CORE_ROWS - VALID, 256), F32)
        vle[q, VALID:, :] = jnp.zeros((CORE_ROWS - VALID, 256), BF16)

    loads[0].wait()
    lacc[...] = vll[...].astype(F32)
    loads[1].wait()
    high, low = split(vpt[...])
    none = jnp.zeros((64, 256), BF16)
    w[0] = jnp.concatenate([high, none], axis=0)
    w[1] = jnp.concatenate([low, none], axis=0)
    w[2] = jnp.concatenate([none, high], axis=0)
    w[3] = jnp.concatenate([none, low], axis=0)
    pl.semaphore_wait(barrier, 4)

    started = []

    def send(src, dst, send_sem, recv_sem, where):
        copy = pltpu.make_async_remote_copy(
            src_ref=src, dst_ref=dst, send_sem=send_sem, recv_sem=recv_sem,
            device_id=where, device_id_type=MESH,
        )
        copy.start()
        started.append(copy)
        return copy

    lcopies = {}

    def lunit(h, c, f1, f2):
        return ((h * LC + c) * 4 + f1 * 2 + f2) * LU

    def lstage(stage, h, c):
        (p1, f1), (p2, f2) = plan[h]
        n = h * LC + c
        i = n * 4 + stage
        if stage == 0:
            src, dst, p = rows(lacc, lunit(h, c, 1 - f1, 0), 2 * LU), lr1.at[pl.ds(n * 2 * LU, 2 * LU)], p1
        elif stage == 1:
            src, dst, p = rows(lacc, lunit(h, c, f1, 1 - f2), LU), lr2.at[pl.ds(n * LU, LU)], p2
        elif stage == 2:
            src = dst = rows(lsum, lunit(h, c, f1, f2), LU)
            p = p2
        else:
            src = dst = rows(lsum, lunit(h, c, f1, 0), 2 * LU)
            p = p1
        lcopies[stage, h, c] = send(src, dst, lsend.at[i], lrecv.at[i], {"groups": p})

    ecopies = {}

    def eunit(k, c, h, f1, f2):
        return (((k * EC + c) * 2 + h) * 4 + f1 * 2 + f2) * EU

    def estage(stage, c, h):
        (p1, f1), (p2, f2) = plan[h]
        n = c * 2 + h
        i = n * 4 + stage
        if stage == 0:
            src, dst, p = rows(pk, eunit(core, c, h, 1 - f1, 0), 2 * EU), er1.at[pl.ds(n * 2 * EU, 2 * EU)], p1
        elif stage == 1:
            src, dst, p = rows(pk, eunit(core, c, h, f1, 1 - f2), EU), er2.at[pl.ds(n * EU, EU)], p2
        elif stage == 2:
            src = dst = rows(esum, eunit(core, c, h, f1, f2), EU)
            p = p2
        else:
            src = dst = rows(esum, eunit(core, c, h, f1, 0), 2 * EU)
            p = p1
        ecopies[stage, c, h] = send(src, dst, esend.at[i], erecv.at[i], {"groups": p})

    def project(k, c):
        @pl.loop(0, 4)
        def _(step):
            start = pl.multiple_of(c * 512 + step * 128, 128)
            total = None
            for side in range(2):
                q = side * 2 + k
                d = vge[q, pl.ds(start, 128), :] - vle[q, pl.ds(start, 128), :].astype(F32)
                dh, dl = split(d)
                part = dot_t(dh, w[side * 2]) + dot_t(dl, w[side * 2]) + dot_t(dh, w[side * 2 + 1])
                total = part if total is None else total + part
            pk[pl.ds(pl.multiple_of(k * CORE_ROWS + start, 128), 128), :] = total

    for c in range(LC):
        for h in range(2):
            lstage(0, h, c)

    ccopies = {}
    for c in range(EC):
        for turn in range(2):
            k = (1 - core) if turn == 0 else core
            for side in range(2):
                for copy in eloads[turn, c, side]:
                    copy.wait()
            project(k, c)
            if turn == 0:
                ccopies[0, c] = send(
                    rows(pk, eunit(k, c, 0, 0, 0), 512), er0.at[pl.ds(c * 512, 512)],
                    csend.at[c], crecv.at[c], other_core,
                )
    for c in range(EC):
        ccopies[0, c].wait_recv()
        mine = pl.ds(pl.multiple_of(eunit(core, c, 0, 0, 0), 8), 512)
        pk[mine, :] += er0[pl.ds(c * 512, 512), :]
        for h in range(2):
            estage(0, c, h)

    for c in range(LC):
        for h in range(2):
            lcopies[0, h, c].wait_recv()
            f1 = plan[h][0][1]
            mine = pl.ds(pl.multiple_of(lunit(h, c, f1, 0), 8), 2 * LU)
            lacc[mine, :] += lr1[pl.ds((h * LC + c) * 2 * LU, 2 * LU), :]
            lstage(1, h, c)

    for c in range(EC):
        for h in range(2):
            ecopies[0, c, h].wait_recv()
            f1 = plan[h][0][1]
            mine = pl.ds(pl.multiple_of(eunit(core, c, h, f1, 0), 8), 2 * EU)
            pk[mine, :] += er1[pl.ds((c * 2 + h) * 2 * EU, 2 * EU), :]
            estage(1, c, h)

    xcopies = {}
    for c in range(EC):
        for h in range(2):
            ecopies[1, c, h].wait_recv()
            (_, f1), (_, f2) = plan[h]
            n = c * 2 + h
            start = eunit(core, c, h, f1, f2)
            mine = pl.ds(pl.multiple_of(start, 8), EU)
            pk[mine, :] += er2[pl.ds(n * EU, EU), :]
            xcopies[c, h] = send(
                rows(pk, start, EU), erx.at[pl.ds(n * EU, EU)], xsend.at[n], xrecv.at[n], other_x
            )

    for c in range(LC):
        for h in range(2):
            lcopies[1, h, c].wait_recv()
            (_, f1), (_, f2) = plan[h]
            mine = pl.ds(pl.multiple_of(lunit(h, c, f1, f2), 8), LU)
            lsum[mine, :] = lacc[mine, :] + lr2[pl.ds((h * LC + c) * LU, LU), :]
            lstage(2, h, c)

    for c in range(EC):
        for h in range(2):
            xcopies[c, h].wait_recv()
            (_, f1), (_, f2) = plan[h]
            n = c * 2 + h
            mine = pl.ds(pl.multiple_of(eunit(core, c, h, f1, f2), 8), EU)
            esum[mine, :] = pk[mine, :] + erx[pl.ds(n * EU, EU), :]
            estage(2, c, h)

    for c in range(EC):
        for h in range(2):
            ecopies[2, c, h].wait_recv()
            estage(3, c, h)

    for c in range(LC):
        for h in range(2):
            lcopies[2, h, c].wait_recv()
            lstage(3, h, c)

    for copy in loads[2:]:
        copy.wait()
    for c in range(EC):
        for h in range(2):
            ecopies[3, c, h].wait_recv()
            n = c * 2 + h
            whole = rows(esum, eunit(core, c, h, 0, 0), 4 * EU)
            ccopies[1, c, h] = send(whole, whole, csend.at[EC + n], crecv.at[EC + n], other_core)
            start, size = part(c * 2 + h)
            for side in range(2):
                one[side, pl.ds(start, size), :], onem[side, pl.ds(start, size), :] = piece_step(
                    esum, w, vge, vem, core, side, start, size
                )
    for c in range(LC):
        for h in range(2):
            lcopies[3, h, c].wait_recv()
    for c in range(EC):
        for h in range(2):
            ccopies[1, c, h].wait_recv()

    for copy in started:
        copy.wait_send()


def body(
    global_layer, local_layer, layer_momentum, global_embed, local_embed, embed_momentum, projection
):
    hbm = pl.BlockSpec(memory_space=pltpu.HBM)
    vmem = pl.BlockSpec(memory_space=pltpu.VMEM)
    dma = pltpu.SemaphoreType.DMA
    layer_shape = global_layer.shape
    held = (
        pltpu.VMEM((LROWS, 128), F32),
        pltpu.VMEM((LROWS, 128), F32),
        pltpu.VMEM((4, CORE_ROWS, 256), F32),
        pltpu.VMEM((4000, 256), F32),
        pltpu.VMEM((4, 128, 256), BF16),
        pltpu.VMEM((LROWS, 128), F32),
        pltpu.VMEM((2 * CORE_ROWS, 128), F32),
        pltpu.VMEM((2, VALID, 256), F32),
        pltpu.VMEM((2, VALID, 256), F32),
    )
    values = pl.pallas_call(
        kernel,
        out_shape=held,
        in_specs=[hbm] * 7,
        out_specs=(vmem,) * len(held),
        scratch_shapes=[
            pltpu.VMEM((LROWS, 128), BF16),
            pltpu.VMEM((4, CORE_ROWS, 256), BF16),
            pltpu.VMEM((64, 256), F32),
            pltpu.VMEM((LROWS, 128), F32),
            pltpu.VMEM((2 * LC * 2 * LU, 128), F32),
            pltpu.VMEM((2 * LC * LU, 128), F32),
            pltpu.VMEM((2 * CORE_ROWS, 128), F32),
            pltpu.VMEM((CORE_ROWS, 128), F32),
            pltpu.VMEM((2 * EC * 2 * EU, 128), F32),
            pltpu.VMEM((2 * EC * EU, 128), F32),
            pltpu.VMEM((2 * EC * EU, 128), F32),
            dma((5,)),
            dma((4 * EC,)),
            dma((4 * EC,)),
            dma((2 * LC * 4,)),
            dma((2 * LC * 4,)),
            dma((2 * EC * 4,)),
            dma((2 * EC * 4,)),
            dma((2 * EC,)),
            dma((2 * EC,)),
            dma((3 * EC,)),
            dma((3 * EC,)),
        ],
        compiler_params=pltpu.CompilerParams(
            collective_id=0, has_side_effects=True, vmem_limit_bytes=40 * 1024 * 1024
        ),
    )(
        *(
            pltpu.with_memory_space_constraint(array, pltpu.HBM)
            for array in (
                local_layer.reshape(LROWS, 128),
                global_layer.reshape(LROWS, 128),
                layer_momentum.reshape(LROWS, 128),
                local_embed.reshape(4000, 256),
                global_embed,
                embed_momentum,
                projection.T,
            )
        )
    )
    nl, nlm, ne, nem = pl.pallas_call(
        write_kernel,
        out_shape=(
            jax.ShapeDtypeStruct((LROWS, 128), F32),
            jax.ShapeDtypeStruct((LROWS, 128), F32),
            jax.ShapeDtypeStruct((4000, 256), F32),
            jax.ShapeDtypeStruct((4000, 256), F32),
        ),
        in_specs=[vmem] * len(held),
        out_specs=(hbm,) * 4,
        scratch_shapes=[
            pltpu.VMEM((LROWS, 128), F32),
            pltpu.VMEM((LROWS, 128), F32),
            pltpu.VMEM((2, VALID, 256), F32),
            pltpu.VMEM((2, VALID, 256), F32),
            dma((26,)),
        ],
        compiler_params=pltpu.CompilerParams(vmem_limit_bytes=40 * 1024 * 1024),
    )(*values)
    return nl.reshape(layer_shape), nlm.reshape(layer_shape), ne, nem


def solution(mesh):
    in_specs = (
        P(None, "tensor", "shards"),
        P("groups", None, "tensor", "shards"),
        P(None, "tensor", "shards"),
        P("shards", "tensor"),
        P("groups", "shards", "tensor"),
        P("shards", "tensor"),
        P("tensor", None),
    )
    out_specs = (
        P(None, "tensor", "shards"),
        P(None, "tensor", "shards"),
        P("shards", "tensor"),
        P("shards", "tensor"),
    )
    return jax.shard_map(body, mesh=mesh, in_specs=in_specs, out_specs=out_specs, check_vma=False)
```

```python
import jax
import jax.numpy as jnp
from jax import lax
from jax.experimental import pallas as pl
from jax.experimental.pallas import tpu as pltpu
from jax.sharding import PartitionSpec as P

MESH = pl.DeviceIdType.MESH
F32 = jnp.float32
BF16 = jnp.bfloat16

momentum_rate = 0.9
outer_rate = 0.7

LROWS = 2112
LC = 3
LU = 88
EC = 2
EU = 64
CORE_ROWS = EC * 2 * 4 * EU
VALID = 1000


def nesterov(weights, momentum, delta):
    moved = momentum_rate * momentum + delta
    return weights - outer_rate * (delta + momentum_rate * moved), moved


def split(value):
    high = value.astype(BF16)
    return high, (value - high.astype(F32)).astype(BF16)


def dot_t(a, b):
    return lax.dot_general(a, b, (((1,), (1,)), ((), ())), preferred_element_type=F32)


def dot(a, b):
    return jnp.dot(a, b, preferred_element_type=F32)


def part(n):
    return n * 256, min(256, VALID - n * 256)


def piece_step(esum, w, vge, vem, k, side, start, size):
    value = esum[pl.ds(pl.multiple_of(k * CORE_ROWS + start, 8), size), :] * 0.25
    vh, vl = split(value)
    delta = dot(vh, w[side * 2]) + dot(vl, w[side * 2]) + dot(vh, w[side * 2 + 1])
    moment = vem[pl.ds(pl.multiple_of(side * 2000 + k * VALID + start, 8), size), :]
    return nesterov(vge[side * 2 + k, pl.ds(start, size), :], moment, delta)


def write_kernel(
    vgl, vlm, vge, vem, w, lsum, esum, one, onem,
    nl, nlm, ne, nem,
    snl, snlm, sne, snem, sem,
):
    core = lax.rem(lax.axis_index("tensor"), 2)
    started = []

    def put(src, dst):
        copy = pltpu.make_async_copy(src, dst, sem.at[len(started)])
        copy.start()
        started.append(copy)

    def place(k, side, start, size):
        return pl.ds(pl.multiple_of(side * 2000 + k * VALID + start, 8), size)

    for side in range(2):
        put(one.at[side], ne.at[place(core, side, 0, VALID)])
        put(onem.at[side], nem.at[place(core, side, 0, VALID)])
    for n in range(4):
        start, size = part(n)
        for side in range(2):
            rows = pl.ds(start, size)
            sne[side, rows, :], snem[side, rows, :] = piece_step(
                esum, w, vge, vem, 1 - core, side, start, size
            )
            put(sne.at[side, rows], ne.at[place(1 - core, side, start, size)])
            put(snem.at[side, rows], nem.at[place(1 - core, side, start, size)])
    for n in range(3):
        block = pl.ds(n * 704, 704)
        weights = vgl[block, :]
        delta = weights - lsum[block, :] * 0.25
        snl[block, :], snlm[block, :] = nesterov(weights, vlm[block, :], delta)
        put(snl.at[block], nl.at[block])
        put(snlm.at[block], nlm.at[block])
    for copy in started:
        copy.wait()


def kernel(
    ll, gl, lm, le, ge, em, pt,
    vgl, vlm, vge, vem, w, lsum, esum, one, onem,
    vll, vle, vpt,
    lacc, lr1, lr2,
    pk, er0, er1, er2, erx,
    load_sem, le_sem, ge_sem, lsend, lrecv, esend, erecv, xsend, xrecv, csend, crecv,
):
    y = lax.axis_index("groups")
    t = lax.axis_index("tensor")
    core = lax.rem(t, 2)
    x_hi = lax.div(t, 2)
    flip = y + 1 - 2 * lax.rem(y, 2)
    mirror = 3 - y
    bit_b = lax.div(y, 2)
    bit_a = lax.rem(bit_b + y, 2)
    plan = (((flip, bit_a), (mirror, bit_b)), ((mirror, bit_b), (flip, bit_a)))
    other_core = {"tensor": x_hi * 2 + 1 - core}
    other_x = {"tensor": (1 - x_hi) * 2 + core}

    def rows(ref, start, size):
        return ref.at[pl.ds(pl.multiple_of(start, 8), size)]

    loads = [
        pltpu.make_async_copy(src, dst, load_sem.at[i])
        for i, (src, dst) in enumerate(((ll, vll), (pt, vpt), (gl, vgl), (lm, vlm), (em, vem)))
    ]
    piece = ((0, 512), (512, VALID - 512))
    eloads = {}
    for turn in range(2):
        k = (1 - core) if turn == 0 else core
        for c in range(EC):
            start, size = piece[c]
            for side in range(2):
                src = pl.ds(pl.multiple_of(side * 2000 + k * VALID + start, 8), size)
                dst = (side * 2 + k, pl.ds(start, size))
                i = (turn * EC + c) * 2 + side
                eloads[turn, c, side] = (
                    pltpu.make_async_copy(le.at[src], vle.at[dst], le_sem.at[i]),
                    pltpu.make_async_copy(ge.at[src], vge.at[dst], ge_sem.at[i]),
                )
    loads[0].start()
    loads[1].start()
    for c in range(EC):
        for turn in range(2):
            for side in range(2):
                for copy in eloads[turn, c, side]:
                    copy.start()
    for copy in loads[2:]:
        copy.start()

    barrier = pltpu.get_barrier_semaphore()
    for where in ({"groups": flip}, {"groups": mirror}, other_core, other_x):
        pl.semaphore_signal(barrier, inc=1, device_id=where, device_id_type=MESH)

    for q in range(4):
        vge[q, VALID:, :] = jnp.zeros((CORE_ROWS - VALID, 256), F32)
        vle[q, VALID:, :] = jnp.zeros((CORE_ROWS - VALID, 256), BF16)

    loads[0].wait()
    lacc[...] = vll[...].astype(F32)
    loads[1].wait()
    high, low = split(vpt[...])
    none = jnp.zeros((64, 256), BF16)
    w[0] = jnp.concatenate([high, none], axis=0)
    w[1] = jnp.concatenate([low, none], axis=0)
    w[2] = jnp.concatenate([none, high], axis=0)
    w[3] = jnp.concatenate([none, low], axis=0)
    pl.semaphore_wait(barrier, 4)

    started = []

    def send(src, dst, send_sem, recv_sem, where):
        copy = pltpu.make_async_remote_copy(
            src_ref=src, dst_ref=dst, send_sem=send_sem, recv_sem=recv_sem,
            device_id=where, device_id_type=MESH,
        )
        copy.start()
        started.append(copy)
        return copy

    lcopies = {}

    def lunit(h, c, f1, f2):
        return ((h * LC + c) * 4 + f1 * 2 + f2) * LU

    def lstage(stage, h, c):
        (p1, f1), (p2, f2) = plan[h]
        n = h * LC + c
        i = n * 4 + stage
        if stage == 0:
            src, dst, p = rows(lacc, lunit(h, c, 1 - f1, 0), 2 * LU), lr1.at[pl.ds(n * 2 * LU, 2 * LU)], p1
        elif stage == 1:
            src, dst, p = rows(lacc, lunit(h, c, f1, 1 - f2), LU), lr2.at[pl.ds(n * LU, LU)], p2
        elif stage == 2:
            src = dst = rows(lsum, lunit(h, c, f1, f2), LU)
            p = p2
        else:
            src = dst = rows(lsum, lunit(h, c, f1, 0), 2 * LU)
            p = p1
        lcopies[stage, h, c] = send(src, dst, lsend.at[i], lrecv.at[i], {"groups": p})

    ecopies = {}

    def eunit(k, c, h, f1, f2):
        return (((k * EC + c) * 2 + h) * 4 + f1 * 2 + f2) * EU

    def estage(stage, c, h):
        (p1, f1), (p2, f2) = plan[h]
        n = c * 2 + h
        i = n * 4 + stage
        if stage == 0:
            src, dst, p = rows(pk, eunit(core, c, h, 1 - f1, 0), 2 * EU), er1.at[pl.ds(n * 2 * EU, 2 * EU)], p1
        elif stage == 1:
            src, dst, p = rows(pk, eunit(core, c, h, f1, 1 - f2), EU), er2.at[pl.ds(n * EU, EU)], p2
        elif stage == 2:
            src = dst = rows(esum, eunit(core, c, h, f1, f2), EU)
            p = p2
        else:
            src = dst = rows(esum, eunit(core, c, h, f1, 0), 2 * EU)
            p = p1
        ecopies[stage, c, h] = send(src, dst, esend.at[i], erecv.at[i], {"groups": p})

    def project(k, c):
        @pl.loop(0, 4)
        def _(step):
            start = pl.multiple_of(c * 512 + step * 128, 128)
            total = None
            for side in range(2):
                q = side * 2 + k
                d = vge[q, pl.ds(start, 128), :] - vle[q, pl.ds(start, 128), :].astype(F32)
                dh, dl = split(d)
                part = dot_t(dh, w[side * 2]) + dot_t(dl, w[side * 2]) + dot_t(dh, w[side * 2 + 1])
                total = part if total is None else total + part
            pk[pl.ds(pl.multiple_of(k * CORE_ROWS + start, 128), 128), :] = total

    for c in range(LC):
        for h in range(2):
            lstage(0, h, c)

    ccopies = {}
    for c in range(EC):
        for turn in range(2):
            k = (1 - core) if turn == 0 else core
            for side in range(2):
                for copy in eloads[turn, c, side]:
                    copy.wait()
            project(k, c)
            if turn == 0:
                ccopies[0, c] = send(
                    rows(pk, eunit(k, c, 0, 0, 0), 512), er0.at[pl.ds(c * 512, 512)],
                    csend.at[c], crecv.at[c], other_core,
                )
    for c in range(EC):
        ccopies[0, c].wait_recv()
        mine = pl.ds(pl.multiple_of(eunit(core, c, 0, 0, 0), 8), 512)
        pk[mine, :] += er0[pl.ds(c * 512, 512), :]
        for h in range(2):
            estage(0, c, h)

    for c in range(LC):
        for h in range(2):
            lcopies[0, h, c].wait_recv()
            f1 = plan[h][0][1]
            mine = pl.ds(pl.multiple_of(lunit(h, c, f1, 0), 8), 2 * LU)
            lacc[mine, :] += lr1[pl.ds((h * LC + c) * 2 * LU, 2 * LU), :]
            lstage(1, h, c)

    for c in range(EC):
        for h in range(2):
            ecopies[0, c, h].wait_recv()
            f1 = plan[h][0][1]
            mine = pl.ds(pl.multiple_of(eunit(core, c, h, f1, 0), 8), 2 * EU)
            pk[mine, :] += er1[pl.ds((c * 2 + h) * 2 * EU, 2 * EU), :]
            estage(1, c, h)

    xcopies = {}
    for c in range(EC):
        for h in range(2):
            ecopies[1, c, h].wait_recv()
            (_, f1), (_, f2) = plan[h]
            n = c * 2 + h
            start = eunit(core, c, h, f1, f2)
            mine = pl.ds(pl.multiple_of(start, 8), EU)
            pk[mine, :] += er2[pl.ds(n * EU, EU), :]
            xcopies[c, h] = send(
                rows(pk, start, EU), erx.at[pl.ds(n * EU, EU)], xsend.at[n], xrecv.at[n], other_x
            )

    for c in range(LC):
        for h in range(2):
            lcopies[1, h, c].wait_recv()
            (_, f1), (_, f2) = plan[h]
            mine = pl.ds(pl.multiple_of(lunit(h, c, f1, f2), 8), LU)
            lsum[mine, :] = lacc[mine, :] + lr2[pl.ds((h * LC + c) * LU, LU), :]
            lstage(2, h, c)

    for c in range(EC):
        for h in range(2):
            xcopies[c, h].wait_recv()
            (_, f1), (_, f2) = plan[h]
            n = c * 2 + h
            mine = pl.ds(pl.multiple_of(eunit(core, c, h, f1, f2), 8), EU)
            esum[mine, :] = pk[mine, :] + erx[pl.ds(n * EU, EU), :]
            estage(2, c, h)

    for c in range(EC):
        for h in range(2):
            ecopies[2, c, h].wait_recv()
            estage(3, c, h)

    for c in range(LC):
        for h in range(2):
            lcopies[2, h, c].wait_recv()
            lstage(3, h, c)

    for copy in loads[2:]:
        copy.wait()
    for c in range(EC):
        for h in range(2):
            ecopies[3, c, h].wait_recv()
            n = c * 2 + h
            whole = rows(esum, eunit(core, c, h, 0, 0), 4 * EU)
            ccopies[1, c, h] = send(whole, whole, csend.at[EC + n], crecv.at[EC + n], other_core)
            start, size = part(c * 2 + h)
            for side in range(2):
                one[side, pl.ds(start, size), :], onem[side, pl.ds(start, size), :] = piece_step(
                    esum, w, vge, vem, core, side, start, size
                )
    for c in range(LC):
        for h in range(2):
            lcopies[3, h, c].wait_recv()
    for c in range(EC):
        for h in range(2):
            ccopies[1, c, h].wait_recv()

    for copy in started:
        copy.wait_send()


def body(
    global_layer, local_layer, layer_momentum, global_embed, local_embed, embed_momentum, projection
):
    hbm = pl.BlockSpec(memory_space=pltpu.HBM)
    vmem = pl.BlockSpec(memory_space=pltpu.VMEM)
    dma = pltpu.SemaphoreType.DMA
    layer_shape = global_layer.shape
    held = (
        pltpu.VMEM((LROWS, 128), F32),
        pltpu.VMEM((LROWS, 128), F32),
        pltpu.VMEM((4, CORE_ROWS, 256), F32),
        pltpu.VMEM((4000, 256), F32),
        pltpu.VMEM((4, 128, 256), BF16),
        pltpu.VMEM((LROWS, 128), F32),
        pltpu.VMEM((2 * CORE_ROWS, 128), F32),
        pltpu.VMEM((2, VALID, 256), F32),
        pltpu.VMEM((2, VALID, 256), F32),
    )
    values = pl.pallas_call(
        kernel,
        out_shape=held,
        in_specs=[hbm] * 7,
        out_specs=(vmem,) * len(held),
        scratch_shapes=[
            pltpu.VMEM((LROWS, 128), BF16),
            pltpu.VMEM((4, CORE_ROWS, 256), BF16),
            pltpu.VMEM((64, 256), F32),
            pltpu.VMEM((LROWS, 128), F32),
            pltpu.VMEM((2 * LC * 2 * LU, 128), F32),
            pltpu.VMEM((2 * LC * LU, 128), F32),
            pltpu.VMEM((2 * CORE_ROWS, 128), F32),
            pltpu.VMEM((CORE_ROWS, 128), F32),
            pltpu.VMEM((2 * EC * 2 * EU, 128), F32),
            pltpu.VMEM((2 * EC * EU, 128), F32),
            pltpu.VMEM((2 * EC * EU, 128), F32),
            dma((5,)),
            dma((4 * EC,)),
            dma((4 * EC,)),
            dma((2 * LC * 4,)),
            dma((2 * LC * 4,)),
            dma((2 * EC * 4,)),
            dma((2 * EC * 4,)),
            dma((2 * EC,)),
            dma((2 * EC,)),
            dma((3 * EC,)),
            dma((3 * EC,)),
        ],
        compiler_params=pltpu.CompilerParams(
            collective_id=0, has_side_effects=True, vmem_limit_bytes=16 * 1024 * 1024
        ),
    )(
        *(
            pltpu.with_memory_space_constraint(array, pltpu.HBM)
            for array in (
                local_layer.reshape(LROWS, 128),
                global_layer.reshape(LROWS, 128),
                layer_momentum.reshape(LROWS, 128),
                local_embed.reshape(4000, 256),
                global_embed,
                embed_momentum,
                projection.T,
            )
        )
    )
    nl, nlm, ne, nem = pl.pallas_call(
        write_kernel,
        out_shape=(
            jax.ShapeDtypeStruct((LROWS, 128), F32),
            jax.ShapeDtypeStruct((LROWS, 128), F32),
            jax.ShapeDtypeStruct((4000, 256), F32),
            jax.ShapeDtypeStruct((4000, 256), F32),
        ),
        in_specs=[vmem] * len(held),
        out_specs=(hbm,) * 4,
        scratch_shapes=[
            pltpu.VMEM((LROWS, 128), F32),
            pltpu.VMEM((LROWS, 128), F32),
            pltpu.VMEM((2, VALID, 256), F32),
            pltpu.VMEM((2, VALID, 256), F32),
            dma((26,)),
        ],
        compiler_params=pltpu.CompilerParams(vmem_limit_bytes=12 * 1024 * 1024),
    )(*values)
    return nl.reshape(layer_shape), nlm.reshape(layer_shape), ne, nem


def solution(mesh):
    in_specs = (
        P(None, "tensor", "shards"),
        P("groups", None, "tensor", "shards"),
        P(None, "tensor", "shards"),
        P("shards", "tensor"),
        P("groups", "shards", "tensor"),
        P("shards", "tensor"),
        P("tensor", None),
    )
    out_specs = (
        P(None, "tensor", "shards"),
        P(None, "tensor", "shards"),
        P("shards", "tensor"),
        P("shards", "tensor"),
    )
    return jax.shard_map(body, mesh=mesh, in_specs=in_specs, out_specs=out_specs, check_vma=False)
```

```python
import jax
import jax.numpy as jnp
from jax import lax
from jax.experimental import pallas as pl
from jax.experimental.pallas import tpu as pltpu
from jax.sharding import PartitionSpec as P

MESH = pl.DeviceIdType.MESH
F32 = jnp.float32
BF16 = jnp.bfloat16

momentum_rate = 0.9
outer_rate = 0.7

LROWS = 2112
LC = 3
LU = 88
EC = 2
EU = 64
CORE_ROWS = EC * 2 * 4 * EU
VALID = 1000


def nesterov(weights, momentum, delta):
    moved = momentum_rate * momentum + delta
    return weights - outer_rate * (delta + momentum_rate * moved), moved


def split(value):
    high = value.astype(BF16)
    return high, (value - high.astype(F32)).astype(BF16)


def dot_t(a, b):
    return lax.dot_general(a, b, (((1,), (1,)), ((), ())), preferred_element_type=F32)


def dot(a, b):
    return jnp.dot(a, b, preferred_element_type=F32)


def write_kernel(vnl, vnlm, vne, vnem, nl, nlm, ne, nem, sem):
    started = []
    for i in range(4):
        for src, dst, size in ((vne, ne, 1000), (vnem, nem, 1000), (vnl, nl, 528), (vnlm, nlm, 528)):
            rows = pl.ds(i * size, size)
            copy = pltpu.make_async_copy(src.at[rows], dst.at[rows], sem.at[len(started)])
            copy.start()
            started.append(copy)
    for copy in started:
        copy.wait()


def kernel(
    ll, gl, lm, le, ge, em, pt,
    nl, nlm, ne, nem,
    vll, vgl, vlm, vle, vge, vem, vpt, w,
    lacc, lr1, lr2, lsum,
    pk, er0, er1, er2, erx, esum,
    load_sem, le_sem, ge_sem, lsend, lrecv, esend, erecv, xsend, xrecv, csend, crecv,
):
    y = lax.axis_index("groups")
    t = lax.axis_index("tensor")
    core = lax.rem(t, 2)
    x_hi = lax.div(t, 2)
    flip = y + 1 - 2 * lax.rem(y, 2)
    mirror = 3 - y
    bit_b = lax.div(y, 2)
    bit_a = lax.rem(bit_b + y, 2)
    plan = (((flip, bit_a), (mirror, bit_b)), ((mirror, bit_b), (flip, bit_a)))
    other_core = {"tensor": x_hi * 2 + 1 - core}
    other_x = {"tensor": (1 - x_hi) * 2 + core}

    def rows(ref, start, size):
        return ref.at[pl.ds(pl.multiple_of(start, 8), size)]

    loads = [
        pltpu.make_async_copy(src, dst, load_sem.at[i])
        for i, (src, dst) in enumerate(((ll, vll), (pt, vpt), (gl, vgl), (lm, vlm), (em, vem)))
    ]
    piece = ((0, 512), (512, VALID - 512))
    eloads = {}
    for turn in range(2):
        k = (1 - core) if turn == 0 else core
        for c in range(EC):
            start, size = piece[c]
            for side in range(2):
                src = pl.ds(pl.multiple_of(side * 2000 + k * VALID + start, 8), size)
                dst = (side * 2 + k, pl.ds(start, size))
                i = (turn * EC + c) * 2 + side
                eloads[turn, c, side] = (
                    pltpu.make_async_copy(le.at[src], vle.at[dst], le_sem.at[i]),
                    pltpu.make_async_copy(ge.at[src], vge.at[dst], ge_sem.at[i]),
                )
    loads[0].start()
    loads[1].start()
    for c in range(EC):
        for turn in range(2):
            for side in range(2):
                for copy in eloads[turn, c, side]:
                    copy.start()
    for copy in loads[2:]:
        copy.start()

    barrier = pltpu.get_barrier_semaphore()
    for where in ({"groups": flip}, {"groups": mirror}, other_core, other_x):
        pl.semaphore_signal(barrier, inc=1, device_id=where, device_id_type=MESH)

    for q in range(4):
        vge[q, VALID:, :] = jnp.zeros((CORE_ROWS - VALID, 256), F32)
        vle[q, VALID:, :] = jnp.zeros((CORE_ROWS - VALID, 256), BF16)

    loads[0].wait()
    lacc[...] = vll[...].astype(F32)
    loads[1].wait()
    high, low = split(vpt[...])
    none = jnp.zeros((64, 256), BF16)
    w[0] = jnp.concatenate([high, none], axis=0)
    w[1] = jnp.concatenate([low, none], axis=0)
    w[2] = jnp.concatenate([none, high], axis=0)
    w[3] = jnp.concatenate([none, low], axis=0)
    pl.semaphore_wait(barrier, 4)

    started = []

    def send(src, dst, send_sem, recv_sem, where):
        copy = pltpu.make_async_remote_copy(
            src_ref=src, dst_ref=dst, send_sem=send_sem, recv_sem=recv_sem,
            device_id=where, device_id_type=MESH,
        )
        copy.start()
        started.append(copy)
        return copy

    lcopies = {}

    def lunit(h, c, f1, f2):
        return ((h * LC + c) * 4 + f1 * 2 + f2) * LU

    def lstage(stage, h, c):
        (p1, f1), (p2, f2) = plan[h]
        n = h * LC + c
        i = n * 4 + stage
        if stage == 0:
            src, dst, p = rows(lacc, lunit(h, c, 1 - f1, 0), 2 * LU), lr1.at[pl.ds(n * 2 * LU, 2 * LU)], p1
        elif stage == 1:
            src, dst, p = rows(lacc, lunit(h, c, f1, 1 - f2), LU), lr2.at[pl.ds(n * LU, LU)], p2
        elif stage == 2:
            src = dst = rows(lsum, lunit(h, c, f1, f2), LU)
            p = p2
        else:
            src = dst = rows(lsum, lunit(h, c, f1, 0), 2 * LU)
            p = p1
        lcopies[stage, h, c] = send(src, dst, lsend.at[i], lrecv.at[i], {"groups": p})

    ecopies = {}

    def eunit(k, c, h, f1, f2):
        return (((k * EC + c) * 2 + h) * 4 + f1 * 2 + f2) * EU

    def estage(stage, c, h):
        (p1, f1), (p2, f2) = plan[h]
        n = c * 2 + h
        i = n * 4 + stage
        if stage == 0:
            src, dst, p = rows(pk, eunit(core, c, h, 1 - f1, 0), 2 * EU), er1.at[pl.ds(n * 2 * EU, 2 * EU)], p1
        elif stage == 1:
            src, dst, p = rows(pk, eunit(core, c, h, f1, 1 - f2), EU), er2.at[pl.ds(n * EU, EU)], p2
        elif stage == 2:
            src = dst = rows(esum, eunit(core, c, h, f1, f2), EU)
            p = p2
        else:
            src = dst = rows(esum, eunit(core, c, h, f1, 0), 2 * EU)
            p = p1
        ecopies[stage, c, h] = send(src, dst, esend.at[i], erecv.at[i], {"groups": p})

    def project(k, c):
        @pl.loop(0, 4)
        def _(step):
            start = pl.multiple_of(c * 512 + step * 128, 128)
            total = None
            for side in range(2):
                q = side * 2 + k
                d = vge[q, pl.ds(start, 128), :] - vle[q, pl.ds(start, 128), :].astype(F32)
                dh, dl = split(d)
                part = dot_t(dh, w[side * 2]) + dot_t(dl, w[side * 2]) + dot_t(dh, w[side * 2 + 1])
                total = part if total is None else total + part
            pk[pl.ds(pl.multiple_of(k * CORE_ROWS + start, 128), 128), :] = total

    def finish(k, c, h):
        size = min(256, VALID - (c * 2 + h) * 256)
        start = (c * 2 + h) * 256
        value = esum[pl.ds(pl.multiple_of(k * CORE_ROWS + start, 8), size), :] * 0.25
        vh, vl = split(value)
        for side in range(2):
            delta = dot(vh, w[side * 2]) + dot(vl, w[side * 2]) + dot(vh, w[side * 2 + 1])
            out = pl.ds(pl.multiple_of(side * 2000 + k * VALID + start, 8), size)
            ne[out, :], nem[out, :] = nesterov(vge[side * 2 + k, pl.ds(start, size), :], vem[out, :], delta)

    for c in range(LC):
        for h in range(2):
            lstage(0, h, c)

    ccopies = {}
    for c in range(EC):
        for turn in range(2):
            k = (1 - core) if turn == 0 else core
            for side in range(2):
                for copy in eloads[turn, c, side]:
                    copy.wait()
            project(k, c)
            if turn == 0:
                ccopies[0, c] = send(
                    rows(pk, eunit(k, c, 0, 0, 0), 512), er0.at[pl.ds(c * 512, 512)],
                    csend.at[c], crecv.at[c], other_core,
                )
    for c in range(EC):
        ccopies[0, c].wait_recv()
        mine = pl.ds(pl.multiple_of(eunit(core, c, 0, 0, 0), 8), 512)
        pk[mine, :] += er0[pl.ds(c * 512, 512), :]
        for h in range(2):
            estage(0, c, h)

    for c in range(LC):
        for h in range(2):
            lcopies[0, h, c].wait_recv()
            f1 = plan[h][0][1]
            mine = pl.ds(pl.multiple_of(lunit(h, c, f1, 0), 8), 2 * LU)
            lacc[mine, :] += lr1[pl.ds((h * LC + c) * 2 * LU, 2 * LU), :]
            lstage(1, h, c)

    for c in range(EC):
        for h in range(2):
            ecopies[0, c, h].wait_recv()
            f1 = plan[h][0][1]
            mine = pl.ds(pl.multiple_of(eunit(core, c, h, f1, 0), 8), 2 * EU)
            pk[mine, :] += er1[pl.ds((c * 2 + h) * 2 * EU, 2 * EU), :]
            estage(1, c, h)

    xcopies = {}
    for c in range(EC):
        for h in range(2):
            ecopies[1, c, h].wait_recv()
            (_, f1), (_, f2) = plan[h]
            n = c * 2 + h
            start = eunit(core, c, h, f1, f2)
            mine = pl.ds(pl.multiple_of(start, 8), EU)
            pk[mine, :] += er2[pl.ds(n * EU, EU), :]
            xcopies[c, h] = send(
                rows(pk, start, EU), erx.at[pl.ds(n * EU, EU)], xsend.at[n], xrecv.at[n], other_x
            )

    for c in range(LC):
        for h in range(2):
            lcopies[1, h, c].wait_recv()
            (_, f1), (_, f2) = plan[h]
            mine = pl.ds(pl.multiple_of(lunit(h, c, f1, f2), 8), LU)
            lsum[mine, :] = lacc[mine, :] + lr2[pl.ds((h * LC + c) * LU, LU), :]
            lstage(2, h, c)

    for c in range(EC):
        for h in range(2):
            xcopies[c, h].wait_recv()
            (_, f1), (_, f2) = plan[h]
            n = c * 2 + h
            mine = pl.ds(pl.multiple_of(eunit(core, c, h, f1, f2), 8), EU)
            esum[mine, :] = pk[mine, :] + erx[pl.ds(n * EU, EU), :]
            estage(2, c, h)

    for c in range(EC):
        for h in range(2):
            ecopies[2, c, h].wait_recv()
            estage(3, c, h)

    for c in range(LC):
        for h in range(2):
            lcopies[2, h, c].wait_recv()
            lstage(3, h, c)

    for copy in loads[2:]:
        copy.wait()
    for c in range(EC):
        for h in range(2):
            ecopies[3, c, h].wait_recv()
            n = c * 2 + h
            whole = rows(esum, eunit(core, c, h, 0, 0), 4 * EU)
            ccopies[1, c, h] = send(whole, whole, csend.at[EC + n], crecv.at[EC + n], other_core)
            finish(core, c, h)
    for c in range(EC):
        for h in range(2):
            ccopies[1, c, h].wait_recv()
            finish(1 - core, c, h)

    for c in range(LC):
        for h in range(2):
            lcopies[3, h, c].wait_recv()
            block = pl.ds((h * LC + c) * 4 * LU, 4 * LU)
            weights = vgl[block, :]
            delta = weights - lsum[block, :] * 0.25
            nl[block, :], nlm[block, :] = nesterov(weights, vlm[block, :], delta)

    for copy in started:
        copy.wait_send()


def body(
    global_layer, local_layer, layer_momentum, global_embed, local_embed, embed_momentum, projection
):
    hbm = pl.BlockSpec(memory_space=pltpu.HBM)
    vmem = pl.BlockSpec(memory_space=pltpu.VMEM)
    dma = pltpu.SemaphoreType.DMA
    layer_shape = global_layer.shape
    held = pl.pallas_call(
        kernel,
        out_shape=(
            pltpu.VMEM((LROWS, 128), F32),
            pltpu.VMEM((LROWS, 128), F32),
            pltpu.VMEM((4000, 256), F32),
            pltpu.VMEM((4000, 256), F32),
        ),
        in_specs=[hbm] * 7,
        out_specs=(vmem,) * 4,
        scratch_shapes=[
            pltpu.VMEM((LROWS, 128), BF16),
            pltpu.VMEM((LROWS, 128), F32),
            pltpu.VMEM((LROWS, 128), F32),
            pltpu.VMEM((4, CORE_ROWS, 256), BF16),
            pltpu.VMEM((4, CORE_ROWS, 256), F32),
            pltpu.VMEM((4000, 256), F32),
            pltpu.VMEM((64, 256), F32),
            pltpu.VMEM((4, 128, 256), BF16),
            pltpu.VMEM((LROWS, 128), F32),
            pltpu.VMEM((2 * LC * 2 * LU, 128), F32),
            pltpu.VMEM((2 * LC * LU, 128), F32),
            pltpu.VMEM((LROWS, 128), F32),
            pltpu.VMEM((2 * CORE_ROWS, 128), F32),
            pltpu.VMEM((CORE_ROWS, 128), F32),
            pltpu.VMEM((2 * EC * 2 * EU, 128), F32),
            pltpu.VMEM((2 * EC * EU, 128), F32),
            pltpu.VMEM((2 * EC * EU, 128), F32),
            pltpu.VMEM((2 * CORE_ROWS, 128), F32),
            dma((5,)),
            dma((4 * EC,)),
            dma((4 * EC,)),
            dma((2 * LC * 4,)),
            dma((2 * LC * 4,)),
            dma((2 * EC * 4,)),
            dma((2 * EC * 4,)),
            dma((2 * EC,)),
            dma((2 * EC,)),
            dma((3 * EC,)),
            dma((3 * EC,)),
        ],
        compiler_params=pltpu.CompilerParams(
            collective_id=0, has_side_effects=True, vmem_limit_bytes=28 * 1024 * 1024
        ),
    )(
        *(
            pltpu.with_memory_space_constraint(array, pltpu.HBM)
            for array in (
                local_layer.reshape(LROWS, 128),
                global_layer.reshape(LROWS, 128),
                layer_momentum.reshape(LROWS, 128),
                local_embed.reshape(4000, 256),
                global_embed,
                embed_momentum,
                projection.T,
            )
        )
    )
    nl, nlm, ne, nem = pl.pallas_call(
        write_kernel,
        out_shape=tuple(jax.ShapeDtypeStruct(value.shape, F32) for value in held),
        in_specs=[vmem] * 4,
        out_specs=(hbm,) * 4,
        scratch_shapes=[dma((16,))],
        compiler_params=pltpu.CompilerParams(vmem_limit_bytes=1024 * 1024),
    )(*held)
    return nl.reshape(layer_shape), nlm.reshape(layer_shape), ne, nem


def solution(mesh):
    in_specs = (
        P(None, "tensor", "shards"),
        P("groups", None, "tensor", "shards"),
        P(None, "tensor", "shards"),
        P("shards", "tensor"),
        P("groups", "shards", "tensor"),
        P("shards", "tensor"),
        P("tensor", None),
    )
    out_specs = (
        P(None, "tensor", "shards"),
        P(None, "tensor", "shards"),
        P("shards", "tensor"),
        P("shards", "tensor"),
    )
    return jax.shard_map(body, mesh=mesh, in_specs=in_specs, out_specs=out_specs, check_vma=False)
```
